128 devices in a mesh: usr: 16 (over z_hi, y, core), itm: 8 (over x, z_lo).
Axes of the slice: x: 4, y: 4, z: 4 (z_hi: 2, z_lo: 2; z = z_hi * 2 + z_lo), core: 2. Of those that a mesh axis runs over, the one named last changes fastest.
Arguments:
- ratings: bfloat16 [16384, 16384], P('usr', 'itm'), may hold values from -6 to 6
- tile_mask: int32 [128, 128], P('usr', 'itm'), may hold values 0 or 1
- counts: int32 [16], P('usr'), may hold values from 256 to 1024
- users: float32 [16384, 256], P(('usr', 'itm')), may hold values from -1.5 to 1.5
- items: float32 [16384, 256], P(('itm', 'usr')), may hold values from -1.5 to 1.5
- user_mom: float32 [16384, 256], P(('usr', 'itm')), may hold values from -6 to 6
- item_mom: float32 [16384, 256], P(('itm', 'usr')), may hold values from -6 to 6
- user_accept: int32 [128], P(('usr', 'itm')), may hold values 0 or 1
- item_accept: int32 [128], P(('itm', 'usr')), may hold values 0 or 1
Outputs:
- users_out: float32 [16384, 256], P(('usr', 'itm'))
- items_out: float32 [16384, 256], P(('itm', 'usr'))
- user_mom_out: float32 [16384, 256], P(('usr', 'itm'))
- item_mom_out: float32 [16384, 256], P(('itm', 'usr'))
The draws below stay inside these ranges and needn't reach their ends.
All inputs are finite; a program needn't handle non-finite values. No bound on the sum of `tile_mask` or of `user_accept` or of `item_accept` on one device may be relied on, other than what follows from the above.
Results may differ from the reference program's by a relative error of at most 0.01.
Values may be sent and summed in bfloat16 or wider, within the bound.
No kernel may reach another device: no remote copies, remote signals or barrier semaphores. Data moves between devices by JAX's collectives and lax.ppermute only.
A program may use at most 64 MiB of HBM per device.

```python
import jax
import jax.numpy as jnp
from jax import lax

K = 256
BLK = 128
UG = 1024
LEAPS = 2
USERS = 16384
ITEMS = 16384
N_USR = 16


def place_ends(array, own_key, low, high):
    place = [jax.random.randint(jax.random.fold_in(own_key, axis), (), 0, length) for axis, length in enumerate(array.shape)]
    main_axis = array.shape.index(max(array.shape))
    neighbour = place[:main_axis] + [(place[main_axis] + 1) % array.shape[main_axis]] + place[main_axis + 1:]
    return array.at[tuple(place)].set(low).at[tuple(neighbour)].set(high)


def level_of(own_key, extent, cuts, smallest, top_value):
    def one(dim, blocks):
        draws = jax.random.uniform(jax.random.fold_in(jax.random.fold_in(own_key, 6), dim), (blocks,), jnp.float32, smallest / len(cuts), top_value / len(cuts))
        return jnp.repeat(jnp.exp(draws), extent[dim] // blocks).reshape((-1,) + (1,) * (len(extent) - dim - 1))

    loudness = one(*cuts[0])
    for cut in cuts[1:]:
        loudness = loudness * one(*cut)
    return loudness


def normal_values(rng, shape, width, most, shards=(), held_as=jnp.bfloat16):
    loudness = level_of(rng, shape, shards, -0.22, 0.18) if shards else 1.0
    entries = jax.random.normal(rng, shape, jnp.float32) * width * loudness
    return jnp.minimum(jnp.maximum(entries, -most), most).astype(held_as)


def setup_inputs(seed: int = 0) -> dict:
    key_of = jax.random.split(jax.random.key(seed), 10)
    ratings = normal_values(key_of[0], (USERS, ITEMS), 1.0, 6.0, ((0, 16), (1, 8)))
    tile_mask = place_ends((jax.random.randint(key_of[1], (USERS // BLK, ITEMS // BLK), 0, 2) < 1).astype(jnp.int32), jax.random.fold_in(key_of[1], 1), 0, 1)
    counts = place_ends(jax.random.randint(key_of[2], (N_USR,), UG // 4, UG + 1), jax.random.fold_in(key_of[2], 1), UG // 4, UG).astype(jnp.int32)
    users = normal_values(key_of[3], (USERS, K), 0.25, 1.5, ((0, 128),), jnp.float32)
    items = normal_values(key_of[4], (ITEMS, K), 0.25, 1.5, ((0, 128),), jnp.float32)
    user_mom = normal_values(key_of[5], (USERS, K), 1.0, 6.0, ((0, 128),), jnp.float32)
    item_mom = normal_values(key_of[6], (ITEMS, K), 1.0, 6.0, ((0, 128),), jnp.float32)
    user_accept = place_ends((jax.random.randint(key_of[7], (USERS // BLK,), 0, 4) < 3).astype(jnp.int32), jax.random.fold_in(key_of[7], 1), 0, 1)
    item_accept = place_ends((jax.random.randint(key_of[8], (ITEMS // BLK,), 0, 4) < 3).astype(jnp.int32), jax.random.fold_in(key_of[8], 1), 0, 1)
    return {"ratings": ratings, "tile_mask": tile_mask, "counts": counts, "users": users, "items": items, "user_mom": user_mom, "item_mom": item_mom, "user_accept": user_accept, "item_accept": item_accept}


step_size = 0.02


def gradients(users, items, ratings, colmask, counts):
    user_bf = users.astype(jnp.bfloat16)
    item_bf = items.astype(jnp.bfloat16)

    def group(carry, index):
        rows = lax.dynamic_slice_in_dim(user_bf, index * UG, UG, 0)
        rated = lax.dynamic_slice_in_dim(ratings, index * UG, UG, 0)
        masks = lax.dynamic_slice_in_dim(colmask, index * (UG // BLK), UG // BLK, 0)
        guess = jnp.dot(rows, item_bf.T, preferred_element_type=jnp.float32)
        alive = (jnp.arange(UG, dtype=jnp.int32) < counts[index]).astype(jnp.float32)
        error = (rated.astype(jnp.float32) - guess).reshape(UG // BLK, BLK, ITEMS) * masks[:, None, :]
        error = (error.reshape(UG, ITEMS) * alive[:, None]).astype(jnp.bfloat16)
        user_term = jnp.dot(error, item_bf, preferred_element_type=jnp.float32)
        item_term = jnp.dot(error.T, rows, preferred_element_type=jnp.float32)
        return carry + item_term, user_term

    item_sum, user_terms = lax.scan(group, jnp.zeros((ITEMS, K), jnp.float32), jnp.arange(N_USR, dtype=jnp.int32))
    return users - user_terms.reshape(USERS, K), items - item_sum


def reference(ratings, tile_mask, counts, users, items, user_mom, item_mom, user_accept, item_accept):
    colmask = jnp.repeat(tile_mask, BLK, axis=1).astype(jnp.float32)
    user_pos, item_pos = users, items
    user_grad, item_grad = gradients(user_pos, item_pos, ratings, colmask, counts)
    for leap in range(LEAPS):
        user_mom = user_mom - 0.5 * step_size * user_grad
        item_mom = item_mom - 0.5 * step_size * item_grad
        user_pos = user_pos + step_size * user_mom
        item_pos = item_pos + step_size * item_mom
        user_grad, item_grad = gradients(user_pos, item_pos, ratings, colmask, counts)
        user_mom = user_mom - 0.5 * step_size * user_grad
        item_mom = item_mom - 0.5 * step_size * item_grad
    user_take = jnp.repeat(user_accept, BLK)[:, None] > 0
    item_take = jnp.repeat(item_accept, BLK)[:, None] > 0
    return jnp.where(user_take, user_pos, users), jnp.where(item_take, item_pos, items), user_mom, item_mom
```

```python
import jax
import jax.numpy as jnp
from jax import lax
from jax.sharding import PartitionSpec as P

BLK = 128
LEAPS = 2
step_size = 0.02
BF = jnp.bfloat16
F32 = jnp.float32


def swap(array, axis, bits):
    size = lax.axis_size(axis)
    return lax.ppermute(array, axis, [(i, i ^ bits) for i in range(size)])


def pick(array, index):
    return lax.dynamic_index_in_dim(array, index, 0, keepdims=False)


def absolute(pieces, index):
    stack = jnp.stack(pieces)
    return jnp.stack([pick(stack, index ^ k) for k in range(len(pieces))])


def body(ratings, tile_mask, counts, users, items, user_mom, item_mom, user_accept, item_accept):
    rows, cols = ratings.shape
    K = users.shape[1]
    u = lax.axis_index("usr")
    i = lax.axis_index("itm")
    zh, y, c = u // 8, (u // 2) % 4, u % 2
    x, zl = i // 2, i % 2
    colmask = jnp.repeat(tile_mask, BLK, axis=1).astype(F32)
    alive = (jnp.arange(rows, dtype=jnp.int32) < counts[0]).astype(F32)

    def compute(full_users, piece):
        guess = jnp.dot(full_users, piece.T, preferred_element_type=F32)
        error = (ratings.astype(F32) - guess).reshape(rows // BLK, BLK, cols) * colmask[:, None, :]
        error = (error.reshape(rows, cols) * alive[:, None]).astype(BF)
        user_sum = jnp.dot(error, piece, preferred_element_type=F32)
        item_sum = jnp.dot(error.T, full_users, preferred_element_type=F32)
        return user_sum.astype(BF), item_sum.astype(BF)

    def gather_users(pair):
        pieces = [pair] + [swap(pair, "itm", 2 * k) for k in (1, 2, 3)]
        return absolute(pieces, x).reshape(rows, K)

    def gather_items(pair):
        pieces = [pair] + [swap(pair, "usr", 2 * k) for k in (1, 2, 3)]
        half = absolute(pieces, y)
        other = swap(half, "usr", 1)
        both = absolute([half, other], c)
        return both.transpose(2, 1, 0, 3, 4).reshape(cols, K)

    def reduce_users(part):
        part = part.reshape(4, 2, BLK, K)
        got = [swap(pick(part, x ^ k), "itm", 2 * k).astype(F32) for k in (1, 2, 3)]
        return (pick(part, x).astype(F32) + got[0] + got[1] + got[2]).astype(BF)

    def reduce_items(part):
        part = part.reshape(2, 4, 2, BLK, K).transpose(2, 1, 0, 3, 4)
        half = pick(part, c).astype(F32) + swap(pick(part, 1 - c), "usr", 1).astype(F32)
        half = half.astype(BF)
        got = [swap(pick(half, y ^ k), "usr", 2 * k).astype(F32) for k in (1, 2, 3)]
        return (pick(half, y).astype(F32) + got[0] + got[1] + got[2]).astype(BF)

    def pair_of(mine, other, z):
        return absolute([mine, other], z)

    def split(pos):
        high = pos.astype(BF)
        return high, (pos - high.astype(F32)).astype(BF)

    uh, ul = split(users)
    vh, vl = split(items)
    uh_o, vh_o = swap(uh, "itm", 1), swap(vh, "usr", 8)
    ul_o, vl_o = swap(jnp.stack([ul, user_mom.astype(BF)]), "itm", 1), swap(jnp.stack([vl, item_mom.astype(BF)]), "usr", 8)
    user_bf, item_bf = pair_of(uh, uh_o, zl), pair_of(vh, vh_o, zh)
    up = pair_of(users, uh_o.astype(F32) + ul_o[0].astype(F32), zl)
    vp = pair_of(items, vh_o.astype(F32) + vl_o[0].astype(F32), zh)
    um = pair_of(user_mom, ul_o[1].astype(F32), zl)
    vm = pair_of(item_mom, vl_o[1].astype(F32), zh)

    half_step = 0.5 * step_size
    for leap in range(LEAPS):
        gu, gv = compute(gather_users(user_bf), gather_items(item_bf))
        su, sv = reduce_users(gu), reduce_items(gv)
        eu = su.astype(F32) + swap(su, "itm", 1).astype(F32)
        ev = sv.astype(F32) + swap(sv, "usr", 8).astype(F32)
        scale = half_step if leap == 0 else 2 * half_step
        um = um - scale * (up - eu)
        vm = vm - scale * (vp - ev)
        up = up + step_size * um
        vp = vp + step_size * vm
        user_bf, item_bf = up.astype(BF), vp.astype(BF)
    gu, gv = compute(gather_users(user_bf), gather_items(item_bf))
    su, sv = reduce_users(gu), reduce_items(gv)
    eu = pick(su, zl).astype(F32) + swap(pick(su, 1 - zl), "itm", 1).astype(F32)
    ev = pick(sv, zh).astype(F32) + swap(pick(sv, 1 - zh), "usr", 8).astype(F32)
    up, vp, um, vm = pick(up, zl), pick(vp, zh), pick(um, zl), pick(vm, zh)
    um = um - half_step * (up - eu)
    vm = vm - half_step * (vp - ev)
    user_take = jnp.repeat(user_accept, BLK)[:, None] > 0
    item_take = jnp.repeat(item_accept, BLK)[:, None] > 0
    return (
        jnp.where(user_take, up, users),
        jnp.where(item_take, vp, items),
        um,
        vm,
    )


def solution(mesh):
    in_specs = (
        P("usr", "itm"),
        P("usr", "itm"),
        P("usr"),
        P(("usr", "itm"), None),
        P(("itm", "usr"), None),
        P(("usr", "itm"), None),
        P(("itm", "usr"), None),
        P(("usr", "itm")),
        P(("itm", "usr")),
    )
    out_specs = (
        P(("usr", "itm"), None),
        P(("itm", "usr"), None),
        P(("usr", "itm"), None),
        P(("itm", "usr"), None),
    )
    return jax.shard_map(body, mesh=mesh, in_specs=in_specs, out_specs=out_specs, check_vma=False)
```

```python
import jax
import jax.numpy as jnp
from jax import lax
from jax.sharding import PartitionSpec as P

BLK = 128
LEAPS = 2
step_size = 0.02
BF = jnp.bfloat16
F32 = jnp.float32


def swap(array, axis, bits):
    size = lax.axis_size(axis)
    return lax.ppermute(array, axis, [(i, i ^ bits) for i in range(size)])


def after(value, *others):
    return lax.optimization_barrier((value, others))[0]


def pick(array, index):
    return lax.dynamic_index_in_dim(array, index, 0, keepdims=False)


def absolute(pieces, index):
    stack = jnp.stack(pieces)
    return jnp.stack([pick(stack, index ^ k) for k in range(len(pieces))])


def body(ratings, tile_mask, counts, users, items, user_mom, item_mom, user_accept, item_accept):
    rows, cols = ratings.shape
    K = users.shape[1]
    u = lax.axis_index("usr")
    i = lax.axis_index("itm")
    zh, y, c = u // 8, (u // 2) % 4, u % 2
    x, zl = i // 2, i % 2
    colmask = jnp.repeat(tile_mask, BLK, axis=1).astype(F32)
    alive = (jnp.arange(rows, dtype=jnp.int32) < counts[0]).astype(F32)

    def errors(full_users, piece):
        guess = jnp.dot(full_users, piece.T, preferred_element_type=F32)
        error = (ratings.astype(F32) - guess).reshape(rows // BLK, BLK, cols) * colmask[:, None, :]
        return (error.reshape(rows, cols) * alive[:, None]).astype(BF)

    def gather(user_pair, item_pair):
        got_v = [swap(item_pair, "usr", 2 * k) for k in (2, 1, 3)]
        got_u = [swap(user_pair, "itm", 2 * k) for k in (2, 1, 3)]
        first = got_u[0]
        got_v = after(got_v, first)
        half = absolute([item_pair, got_v[1], got_v[0], got_v[2]], y)
        other = swap(half, "usr", 1)
        full_users = absolute([user_pair, got_u[1], got_u[0], got_u[2]], x).reshape(rows, K)
        both = absolute([half, after(other, full_users)], c)
        return full_users, both.transpose(2, 1, 0, 3, 4).reshape(cols, K)

    def reduce(error, full_users, piece):
        part = jnp.dot(error.T, full_users, preferred_element_type=F32).astype(BF)
        part = part.reshape(2, 4, 2, BLK, K).transpose(2, 1, 0, 3, 4)
        other = swap(pick(part, 1 - c), "usr", 1)
        user_part = jnp.dot(after(error, part), piece, preferred_element_type=F32).astype(BF)
        user_part = user_part.reshape(4, 2, BLK, K)
        other, user_part = lax.optimization_barrier((other, user_part))
        half = (pick(part, c).astype(F32) + other.astype(F32)).astype(BF)
        got_v = [swap(pick(half, y ^ k), "usr", 2 * k) for k in (2, 1, 3)]
        got_u = [swap(pick(user_part, x ^ k), "itm", 2 * k) for k in (2, 1, 3)]
        got_v = after(got_v, got_u[0])
        item_sum = pick(half, y).astype(F32)
        for got in got_v:
            item_sum += got.astype(F32)
        user_sum = pick(user_part, x).astype(F32)
        for got in got_u:
            user_sum += got.astype(F32)
        return user_sum.astype(BF), item_sum.astype(BF)

    def pair_of(mine, other, z):
        return absolute([mine, other], z)

    def split(pos):
        high = pos.astype(BF)
        return high, (pos - high.astype(F32)).astype(BF)

    uh, ul = split(users)
    vh, vl = split(items)
    uh_o, vh_o = swap(uh, "itm", 1), swap(vh, "usr", 8)
    ul_o, vl_o = swap(jnp.stack([ul, user_mom.astype(BF)]), "itm", 1), swap(jnp.stack([vl, item_mom.astype(BF)]), "usr", 8)
    user_bf, item_bf = pair_of(uh, uh_o, zl), pair_of(vh, vh_o, zh)
    up = pair_of(users, uh_o.astype(F32) + ul_o[0].astype(F32), zl)
    vp = pair_of(items, vh_o.astype(F32) + vl_o[0].astype(F32), zh)
    um = pair_of(user_mom, ul_o[1].astype(F32), zl)
    vm = pair_of(item_mom, vl_o[1].astype(F32), zh)

    half_step = 0.5 * step_size
    for leap in range(LEAPS):
        full_users, piece = gather(user_bf, item_bf)
        su, sv = reduce(errors(full_users, piece), full_users, piece)
        eu = su.astype(F32) + swap(su, "itm", 1).astype(F32)
        ev = sv.astype(F32) + swap(sv, "usr", 8).astype(F32)
        scale = half_step if leap == 0 else 2 * half_step
        um = um - scale * (up - eu)
        vm = vm - scale * (vp - ev)
        up = up + step_size * um
        vp = vp + step_size * vm
        user_bf, item_bf = up.astype(BF), vp.astype(BF)
    full_users, piece = gather(user_bf, item_bf)
    su, sv = reduce(errors(full_users, piece), full_users, piece)
    eu = pick(su, zl).astype(F32) + swap(pick(su, 1 - zl), "itm", 1).astype(F32)
    ev = pick(sv, zh).astype(F32) + swap(pick(sv, 1 - zh), "usr", 8).astype(F32)
    up, vp, um, vm = pick(up, zl), pick(vp, zh), pick(um, zl), pick(vm, zh)
    um = um - half_step * (up - eu)
    vm = vm - half_step * (vp - ev)
    user_take = jnp.repeat(user_accept, BLK)[:, None] > 0
    item_take = jnp.repeat(item_accept, BLK)[:, None] > 0
    return (
        jnp.where(user_take, up, users),
        jnp.where(item_take, vp, items),
        um,
        vm,
    )


def solution(mesh):
    in_specs = (
        P("usr", "itm"),
        P("usr", "itm"),
        P("usr"),
        P(("usr", "itm"), None),
        P(("itm", "usr"), None),
        P(("usr", "itm"), None),
        P(("itm", "usr"), None),
        P(("usr", "itm")),
        P(("itm", "usr")),
    )
    out_specs = (
        P(("usr", "itm"), None),
        P(("itm", "usr"), None),
        P(("usr", "itm"), None),
        P(("itm", "usr"), None),
    )
    return jax.shard_map(body, mesh=mesh, in_specs=in_specs, out_specs=out_specs, check_vma=False)
```
